32 devices in a mesh: dp: 16 (over z, x, core), axial: 2 (over y).
Axes of the slice: x: 2, y: 2, z: 4, core: 2. Of those that a mesh axis runs over, the one named last changes fastest.
Arguments:
- homolog_activations: bfloat16 [16, 32, 16, 256], P('dp', None, 'axial'), may hold values from -6 to 6
- homolog_adjoint: bfloat16 [16, 32, 16, 256], P('dp', None, 'axial'), may hold values from -6 to 6
- duplex_adjoint: bfloat16 [16, 16, 16, 128], P('dp', 'axial'), may hold values from -6 to 6
- homolog_exists_filter: int32 [16, 32], P('dp'), may hold values 0 or 1
- amino_exists_filter: int32 [16, 16], P('dp'), may hold values 0 or 1
- focus_matrices_tier: bfloat16 [5, 256, 256], replicated, may hold values from -0.375 to 0.375
- affine_parameters: float32 [5, 256], replicated, may hold values from -1.5 to 1.75, as said below
- left_right_matrices: bfloat16 [256, 64], replicated, may hold values from -0.375 to 0.375
- outer_final_matrix: bfloat16 [1024, 128], replicated, may hold values from -0.1875 to 0.1875
Outputs:
- homolog_derivative: bfloat16 [16, 32, 16, 256], P('dp', None, 'axial')
- grad_attention: float32 [5, 256, 256], replicated
- grad_vectors: float32 [5, 256], replicated
- grad_proj: float32 [256, 64], replicated
- pair_weight_gradient: float32 [1024, 128], replicated
The draws below stay inside these ranges and needn't reach their ends.
Inputs may be any that keep to these rules, and one draw needn't show every extreme that they name: `affine_parameters`: gains near one, biases near zero.
All inputs are finite; a program needn't handle non-finite values. No bound on the sum of `homolog_exists_filter` or of `amino_exists_filter` on one device may be relied on, other than what follows from the above.
Results may differ from the reference program's by a relative error of at most 0.018.
Values may be sent and summed in bfloat16 or wider, within the bound.
No kernel may reach another device: no remote copies, remote signals or barrier semaphores. Data moves between devices by JAX's collectives and lax.ppermute only.
A program may use at most 64 MiB of HBM per device.

```python
from functools import partial
import jax
import jax.numpy as jnp
from jax import lax

HOMOLOG_FEATURES = 256
HEADS = 8
HEAD_DIM = 32
OUTER_FACTORS = 32
DUPLEX_FEATURES = 128
HOMOLOG_NUMBER = 32
LOCAL_RESIDUES = 8
AMINO_SITES = 16
PROTEIN_NUMBER = 16
N_AXIAL = 2


def draw_affine_parameters(key, part):
    random_jitter = jnp.clip(jax.random.normal(key, (5, HOMOLOG_FEATURES), jnp.float32), -3.0, 3.0)
    centers = jnp.array([1.0, 0.0, 0.0, 1.0, 0.0], jnp.float32)[:, None]
    spreads = jnp.array([0.25, 0.5, 0.5, 0.25, 0.5], jnp.float32)[:, None]
    return centers + spreads * random_jitter


def set_ends(result, stream_key, low, largest):
    place = [jax.random.randint(jax.random.fold_in(stream_key, axis), (), 0, length) for axis, length in enumerate(result.shape)]
    main_axis = result.shape.index(max(result.shape))
    beside = place[:main_axis] + [(place[main_axis] + 1) % result.shape[main_axis]] + place[main_axis + 1:]
    return result.at[tuple(place)].set(low).at[tuple(beside)].set(largest)


def level_of(rng, extent, pieces, low, largest):
    def one(axis_at, parts):
        heights = jax.random.uniform(jax.random.fold_in(jax.random.fold_in(rng, 6), axis_at), (parts,), jnp.float32, low / len(pieces), largest / len(pieces))
        return jnp.repeat(jnp.exp(heights), extent[axis_at] // parts).reshape((-1,) + (1,) * (len(extent) - axis_at - 1))

    loudness = one(*pieces[0])
    for cut in pieces[1:]:
        loudness = loudness * one(*cut)
    return loudness


def noise(rng, shape, scale, bound, cuts=(), held_as=jnp.bfloat16):
    drawn = jax.random.normal(rng, shape, jnp.float32) * scale
    if len(cuts) > 0:
        drawn = level_of(rng, shape, cuts, -0.22, 0.18) * drawn
    return jnp.clip(drawn, min=-bound, max=bound).astype(held_as)


def setup_inputs(seed: int = 0) -> dict:
    keys = jax.random.split(jax.random.key(seed), 10)
    return {
        "homolog_activations": noise(keys[0], (PROTEIN_NUMBER, HOMOLOG_NUMBER, AMINO_SITES, HOMOLOG_FEATURES), 1.0, 6.0, ((0, 16), (2, 2))),
        "homolog_adjoint": noise(keys[1], (PROTEIN_NUMBER, HOMOLOG_NUMBER, AMINO_SITES, HOMOLOG_FEATURES), 1.0, 6.0, ((0, 16), (2, 2))),
        "duplex_adjoint": noise(keys[2], (PROTEIN_NUMBER, AMINO_SITES, AMINO_SITES, DUPLEX_FEATURES), 1.0, 6.0, ((0, 16), (1, 2))),
        "homolog_exists_filter": set_ends((jax.random.randint(keys[3], (PROTEIN_NUMBER, HOMOLOG_NUMBER), 0, 8) < 7).astype(jnp.int32), jax.random.fold_in(keys[3], 1), 0, 1),
        "amino_exists_filter": set_ends((jax.random.randint(keys[4], (PROTEIN_NUMBER, AMINO_SITES), 0, 8) < 7).astype(jnp.int32), jax.random.fold_in(keys[4], 1), 0, 1),
        "focus_matrices_tier": noise(keys[5], (5, HOMOLOG_FEATURES, HOMOLOG_FEATURES), HOMOLOG_FEATURES ** -0.5, 0.375),
        "affine_parameters": draw_affine_parameters(jax.random.fold_in(keys[9], 71), 0),
        "left_right_matrices": noise(keys[7], (HOMOLOG_FEATURES, 2 * OUTER_FACTORS), HOMOLOG_FEATURES ** -0.5, 0.375),
        "outer_final_matrix": noise(keys[8], (OUTER_FACTORS * OUTER_FACTORS, DUPLEX_FEATURES), (OUTER_FACTORS * OUTER_FACTORS) ** -0.5, 0.1875),
    }


def layer_normalize(values, scale_row, shift_row):
    average = lax.optimization_barrier(jnp.mean(values, axis=-1, keepdims=True))
    centered = values - average
    spread = lax.optimization_barrier(jnp.mean(centered * centered, axis=-1, keepdims=True))
    return centered * lax.rsqrt(spread + 1e-05) * scale_row + shift_row

def column_attention_block(sequence_flags, residue_flags, alignment_block, focus_matrices_tier, affine_parameters, left_right_matrices):
    sequence_total, present_row_count, channel_width = alignment_block.shape
    normalized_input = layer_normalize(alignment_block.astype(jnp.float32), affine_parameters[0], affine_parameters[1]).astype(jnp.bfloat16)
    flat_rows = normalized_input.reshape(sequence_total * present_row_count, channel_width)
    shape_heads = (sequence_total, present_row_count, HEADS, HEAD_DIM)
    queries = (jnp.dot(flat_rows, focus_matrices_tier[0], preferred_element_type=jnp.float32) * HEAD_DIM ** (-0.5)).astype(jnp.bfloat16).reshape(shape_heads)
    keys_all = jnp.dot(flat_rows, focus_matrices_tier[1], preferred_element_type=jnp.float32).astype(jnp.bfloat16).reshape(shape_heads)
    values_all = jnp.dot(flat_rows, focus_matrices_tier[2], preferred_element_type=jnp.float32).astype(jnp.bfloat16).reshape(shape_heads)
    gate_value = jax.nn.sigmoid(jnp.dot(flat_rows, focus_matrices_tier[3], preferred_element_type=jnp.float32) + affine_parameters[2])
    logits = jnp.einsum('srhd,trhd->rhst', queries, keys_all, preferred_element_type=jnp.float32)
    mask_bias = (sequence_flags.astype(jnp.float32) - 1.0) * 1000000000.0
    probs = jax.nn.softmax(logits + mask_bias[None, None, None, :], axis=-1).astype(jnp.bfloat16)
    attended = jnp.einsum('rhst,trhd->srhd', probs, values_all, preferred_element_type=jnp.float32)
    gated = (attended.reshape(sequence_total * present_row_count, channel_width) * gate_value).astype(jnp.bfloat16)
    rows_update = jnp.dot(gated, focus_matrices_tier[4], preferred_element_type=jnp.float32)
    updated_alignment = alignment_block.astype(jnp.float32) + rows_update.reshape(sequence_total, present_row_count, channel_width)
    second = layer_normalize(updated_alignment, affine_parameters[3], affine_parameters[4]).astype(jnp.bfloat16).reshape(sequence_total * present_row_count, channel_width)
    projected = jnp.dot(second, left_right_matrices, preferred_element_type=jnp.float32).reshape(sequence_total, present_row_count, 2 * OUTER_FACTORS)
    flags = (sequence_flags[:, None] * residue_flags[None, :]).astype(jnp.float32)
    projected = (projected * flags[:, :, None]).astype(jnp.bfloat16)
    return (updated_alignment, projected[:, :, :OUTER_FACTORS], projected[:, :, OUTER_FACTORS:])

def pair_block(left_part, right_part, outer_final_matrix, flags_rows, flags_cols, seq_total):
    outer = jnp.einsum('sic,sje->ijce', left_part, right_part, precision=lax.Precision.HIGHEST)
    rows_i, cols_j = (outer.shape[0], outer.shape[1])
    outer_flat = outer.reshape(rows_i * cols_j, OUTER_FACTORS * OUTER_FACTORS).astype(jnp.bfloat16)
    pair_rows = jnp.dot(outer_flat, outer_final_matrix, preferred_element_type=jnp.float32).reshape(rows_i, cols_j, DUPLEX_FEATURES)
    divisor = jnp.maximum(flags_rows[:, None] * flags_cols[None, :] * seq_total, 1.0)
    return pair_rows / divisor[:, :, None]

def reference(homolog_activations, homolog_adjoint, duplex_adjoint, homolog_exists_filter, amino_exists_filter, focus_matrices_tier, affine_parameters, left_right_matrices, outer_final_matrix):

    def single_structure(single_alignment, single_cotangent, pair_update_cotangent, sequence_flags, residue_flags):
        seq_total = jnp.sum(sequence_flags.astype(jnp.float32))
        res_float = residue_flags.astype(jnp.float32)
        backward_results = []
        lefts = []
        rights = []
        for current_block_index in range(N_AXIAL):
            leading_row = current_block_index * LOCAL_RESIDUES
            local_function = partial(column_attention_block, sequence_flags, residue_flags[leading_row:leading_row + LOCAL_RESIDUES])
            step_outputs, backward_function = jax.vjp(local_function, single_alignment[:, leading_row:leading_row + LOCAL_RESIDUES], focus_matrices_tier, affine_parameters, left_right_matrices)
            backward_results.append(backward_function)
            lefts.append(step_outputs[1])
            rights.append(step_outputs[2])
        left_all, right_all = lax.optimization_barrier((jnp.concatenate(lefts, 1), jnp.concatenate(rights, 1)))
        left_float = left_all.astype(jnp.float32)
        right_float = right_all.astype(jnp.float32)
        right_sum = jnp.zeros((HOMOLOG_NUMBER, AMINO_SITES, OUTER_FACTORS), jnp.float32)
        pair_weight_gradient = jnp.zeros((OUTER_FACTORS * OUTER_FACTORS, DUPLEX_FEATURES), jnp.float32)
        left_grads = []
        for current_block_index in range(N_AXIAL):
            leading_row = current_block_index * LOCAL_RESIDUES
            rows_flags = res_float[leading_row:leading_row + LOCAL_RESIDUES]

            def pair_fn(left_part, right_part, weight_part):
                return pair_block(left_part, right_part, weight_part, rows_flags, res_float, seq_total)
            unused, back_pair = jax.vjp(pair_fn, left_float[:, leading_row:leading_row + LOCAL_RESIDUES], right_float, outer_final_matrix)
            left_cot, right_cot, pair_weight_cot = back_pair(pair_update_cotangent[leading_row:leading_row + LOCAL_RESIDUES].astype(jnp.float32))
            right_sum = right_sum + right_cot
            pair_weight_gradient = pair_weight_gradient + pair_weight_cot.astype(jnp.float32)
            left_grads.append(left_cot.astype(jnp.bfloat16))
        right_grad = right_sum.astype(jnp.bfloat16)
        focus_derivative = jnp.zeros((5, HOMOLOG_FEATURES, HOMOLOG_FEATURES), jnp.float32)
        affine_derivative = jnp.zeros((5, HOMOLOG_FEATURES), jnp.float32)
        factor_derivative = jnp.zeros((HOMOLOG_FEATURES, 2 * OUTER_FACTORS), jnp.float32)
        alignment_pieces = []
        for current_block_index in range(N_AXIAL):
            leading_row = current_block_index * LOCAL_RESIDUES
            cotangent_list = (single_cotangent[:, leading_row:leading_row + LOCAL_RESIDUES].astype(jnp.float32), left_grads[current_block_index], right_grad[:, leading_row:leading_row + LOCAL_RESIDUES])
            alignment_piece, attention_piece, vector_piece, projection_piece = backward_results[current_block_index](cotangent_list)
            alignment_pieces.append(alignment_piece)
            focus_derivative = focus_derivative + attention_piece.astype(jnp.float32)
            affine_derivative = affine_derivative + vector_piece.astype(jnp.float32)
            factor_derivative = factor_derivative + projection_piece.astype(jnp.float32)
        return (jnp.concatenate(alignment_pieces, 1), focus_derivative, affine_derivative, factor_derivative, pair_weight_gradient)

    def scan_body_routine(loop_carry, loop_items):
        alignment_piece, focus_derivative, affine_derivative, factor_derivative, pair_weight_gradient = single_structure(*loop_items)
        return ((loop_carry[0] + focus_derivative, loop_carry[1] + affine_derivative, loop_carry[2] + factor_derivative, loop_carry[3] + pair_weight_gradient), alignment_piece)
    starting_state = (jnp.zeros((5, HOMOLOG_FEATURES, HOMOLOG_FEATURES), jnp.float32), jnp.zeros((5, HOMOLOG_FEATURES), jnp.float32), jnp.zeros((HOMOLOG_FEATURES, 2 * OUTER_FACTORS), jnp.float32), jnp.zeros((OUTER_FACTORS * OUTER_FACTORS, DUPLEX_FEATURES), jnp.float32))
    derivative_sums, homolog_derivative = lax.scan(scan_body_routine, starting_state, (homolog_activations, homolog_adjoint, duplex_adjoint, homolog_exists_filter, amino_exists_filter))
    return (homolog_derivative, derivative_sums[0], derivative_sums[1], derivative_sums[2], derivative_sums[3])
```

```python
from functools import partial

import jax
import jax.numpy as jnp
from jax import lax
from jax.sharding import PartitionSpec as P

HEADS = 8
HEAD_DIM = 32
OUTER_FACTORS = 32
DUPLEX_FEATURES = 128


def layer_normalize(values, scale_row, shift_row):
    average = jnp.mean(values, axis=-1, keepdims=True)
    centered = values - average
    spread = jnp.mean(centered * centered, axis=-1, keepdims=True)
    return centered * lax.rsqrt(spread + 1e-05) * scale_row + shift_row


def column_attention_block(
    sequence_flags,
    residue_flags,
    alignment_block,
    focus_matrices_tier,
    affine_parameters,
    left_right_matrices,
):
    sequence_total, present_row_count, channel_width = alignment_block.shape
    normalized_input = layer_normalize(
        alignment_block.astype(jnp.float32), affine_parameters[0], affine_parameters[1]
    ).astype(jnp.bfloat16)
    flat_rows = normalized_input.reshape(sequence_total * present_row_count, channel_width)
    shape_heads = (sequence_total, present_row_count, HEADS, HEAD_DIM)
    queries = (
        (
            jnp.dot(flat_rows, focus_matrices_tier[0], preferred_element_type=jnp.float32)
            * HEAD_DIM ** (-0.5)
        )
        .astype(jnp.bfloat16)
        .reshape(shape_heads)
    )
    keys_all = (
        jnp.dot(flat_rows, focus_matrices_tier[1], preferred_element_type=jnp.float32)
        .astype(jnp.bfloat16)
        .reshape(shape_heads)
    )
    values_all = (
        jnp.dot(flat_rows, focus_matrices_tier[2], preferred_element_type=jnp.float32)
        .astype(jnp.bfloat16)
        .reshape(shape_heads)
    )
    gate_value = jax.nn.sigmoid(
        jnp.dot(flat_rows, focus_matrices_tier[3], preferred_element_type=jnp.float32)
        + affine_parameters[2]
    )
    logits = jnp.einsum("srhd,trhd->rhst", queries, keys_all, preferred_element_type=jnp.float32)
    mask_bias = (sequence_flags.astype(jnp.float32) - 1.0) * 1000000000.0
    probs = jax.nn.softmax(logits + mask_bias[None, None, None, :], axis=-1).astype(jnp.bfloat16)
    attended = jnp.einsum("rhst,trhd->srhd", probs, values_all, preferred_element_type=jnp.float32)
    gated = (
        attended.reshape(sequence_total * present_row_count, channel_width) * gate_value
    ).astype(jnp.bfloat16)
    rows_update = jnp.dot(gated, focus_matrices_tier[4], preferred_element_type=jnp.float32)
    updated_alignment = alignment_block.astype(jnp.float32) + rows_update.reshape(
        sequence_total, present_row_count, channel_width
    )
    second = (
        layer_normalize(updated_alignment, affine_parameters[3], affine_parameters[4])
        .astype(jnp.bfloat16)
        .reshape(sequence_total * present_row_count, channel_width)
    )
    projected = jnp.dot(second, left_right_matrices, preferred_element_type=jnp.float32).reshape(
        sequence_total, present_row_count, 2 * OUTER_FACTORS
    )
    flags = (sequence_flags[:, None] * residue_flags[None, :]).astype(jnp.float32)
    projected = (projected * flags[:, :, None]).astype(jnp.bfloat16)
    return (updated_alignment, projected[:, :, :OUTER_FACTORS], projected[:, :, OUTER_FACTORS:])


def pair_block(left_part, right_part, outer_final_matrix, flags_rows, flags_cols, seq_total):
    outer = jnp.einsum("sic,sje->ijce", left_part, right_part, precision=lax.Precision.HIGHEST)
    rows_i, cols_j = (outer.shape[0], outer.shape[1])
    outer_flat = outer.reshape(rows_i * cols_j, OUTER_FACTORS * OUTER_FACTORS).astype(jnp.bfloat16)
    pair_rows = jnp.dot(outer_flat, outer_final_matrix, preferred_element_type=jnp.float32).reshape(
        rows_i, cols_j, DUPLEX_FEATURES
    )
    divisor = jnp.maximum(flags_rows[:, None] * flags_cols[None, :] * seq_total, 1.0)
    return pair_rows / divisor[:, :, None]


def exchange(value, axes, total, offset):
    return lax.ppermute(value, axes, [(i, i ^ offset) for i in range(total)])


def reduce_gradients(parts, dp_size, axial_size):
    axes = ("dp", "axial")
    if axial_size != 2 or dp_size != 16:
        return lax.psum(parts, axes)
    total = dp_size * axial_size
    flat = jnp.concatenate([p.reshape(-1, 128) for p in parts], axis=0)
    used = flat.shape[0]
    rows = -(-used // 128) * 128
    flat = jnp.pad(flat, ((0, rows - used), (0, 0)))
    index = lax.axis_index(axes)
    core = (index // 2) % 2
    half = rows // 2
    keep = lax.dynamic_slice_in_dim(flat, core * half, half)
    send = lax.dynamic_slice_in_dim(flat, (1 - core) * half, half)
    mine = keep + exchange(send.astype(jnp.bfloat16), axes, total, 2).astype(jnp.float32)
    place = (index % 2) + 2 * ((index // 4) % 2)
    offsets = (1, 4, 5)
    quarter = half // 4
    own = lax.dynamic_slice_in_dim(mine, place * quarter, quarter)
    got = []
    for step, offset in zip((1, 2, 3), offsets):
        piece = lax.dynamic_slice_in_dim(mine, (place ^ step) * quarter, quarter)
        got.append(exchange(piece.astype(jnp.bfloat16), axes, total, offset))
    own = own + got[0].astype(jnp.float32) + got[1].astype(jnp.float32) + got[2].astype(jnp.float32)
    own = own.astype(jnp.bfloat16)
    level = [exchange(own, axes, total, offset).astype(jnp.float32) for offset in (8, 16, 24)]
    own = ((own.astype(jnp.float32) + level[0]) + (level[1] + level[2])).astype(jnp.bfloat16)
    pieces = [own] + [exchange(own, axes, total, offset) for offset in offsets]
    stacked = jnp.stack(pieces)
    mine = jnp.concatenate([lax.dynamic_index_in_dim(stacked, place ^ k, keepdims=False) for k in range(4)], axis=0)
    other = exchange(mine, axes, total, 2)
    both = jnp.concatenate(
        [jnp.where(core == 0, mine, other), jnp.where(core == 0, other, mine)], axis=0
    ).astype(jnp.float32)
    outs, at = [], 0
    for p in parts:
        n = p.size // 128
        outs.append(both[at : at + n].reshape(p.shape))
        at += n
    return tuple(outs)


def per_device(
    dp_size,
    axial_size,
    homolog_activations,
    homolog_adjoint,
    duplex_adjoint,
    homolog_exists_filter,
    amino_exists_filter,
    focus_matrices_tier,
    affine_parameters,
    left_right_matrices,
    outer_final_matrix,
):
    shard_homologs = homolog_activations[0]
    local_cotangent = homolog_adjoint[0]
    pair_update_cotangent = duplex_adjoint[0]
    sequence_flags = homolog_exists_filter[0]
    residue_flags = amino_exists_filter[0]
    present_row_count = shard_homologs.shape[1]
    own_index = lax.axis_index("axial")
    own_flags = lax.dynamic_slice_in_dim(
        residue_flags, own_index * present_row_count, present_row_count
    )
    seq_total = jnp.sum(sequence_flags.astype(jnp.float32))
    res_float = residue_flags.astype(jnp.float32)
    own_float = own_flags.astype(jnp.float32)
    local_function = partial(column_attention_block, sequence_flags, own_flags)
    step_outputs, backward_function = jax.vjp(
        local_function, shard_homologs, focus_matrices_tier, affine_parameters, left_right_matrices
    )
    left_own, right_own = lax.optimization_barrier((step_outputs[1], step_outputs[2]))
    left_float = left_own.astype(jnp.float32)
    right_all = lax.all_gather(right_own, "axial", axis=1, tiled=True)

    def pair_fn(left_part, right_part, weight_part):
        return pair_block(left_part, right_part, weight_part, own_float, res_float, seq_total)

    unused, back_pair = jax.vjp(
        pair_fn, left_float, right_all.astype(jnp.float32), outer_final_matrix
    )
    left_cot, right_cot, pair_weight_cot = back_pair(pair_update_cotangent.astype(jnp.float32))
    right_grad = lax.psum_scatter(
        right_cot.astype(jnp.bfloat16), "axial", scatter_dimension=1, tiled=True
    )
    pair_weight_gradient = pair_weight_cot.astype(jnp.float32)
    cotangent_list = (
        local_cotangent.astype(jnp.float32),
        left_cot.astype(jnp.bfloat16),
        right_grad,
    )
    alignment_piece, attention_piece, vector_piece, projection_piece = backward_function(
        cotangent_list
    )
    focus_derivative = attention_piece.astype(jnp.float32)
    affine_derivative = vector_piece
    factor_derivative = projection_piece.astype(jnp.float32)
    focus_derivative, affine_derivative, factor_derivative, pair_weight_gradient = reduce_gradients(
        (focus_derivative, affine_derivative, factor_derivative, pair_weight_gradient),
        dp_size,
        axial_size,
    )
    return (
        alignment_piece[None],
        focus_derivative,
        affine_derivative,
        factor_derivative,
        pair_weight_gradient,
    )


def solution(mesh):
    return jax.shard_map(
        partial(per_device, mesh.shape["dp"], mesh.shape["axial"]),
        mesh=mesh,
        in_specs=(
            P("dp", None, "axial", None),
            P("dp", None, "axial", None),
            P("dp", "axial", None, None),
            P("dp", None),
            P("dp", None),
            P(),
            P(),
            P(),
            P(),
        ),
        out_specs=(P("dp", None, "axial", None), P(), P(), P(), P()),
        check_vma=False,
    )
```

```python
from functools import partial

import jax
import jax.numpy as jnp
from jax import lax
from jax.experimental import pallas as pl
from jax.experimental.pallas import tpu as pltpu
from jax.sharding import PartitionSpec as P

HEADS = 8
HEAD_DIM = 32
OUTER_FACTORS = 32
DUPLEX_FEATURES = 128
BF = jnp.bfloat16
F32 = jnp.float32


def mm(a, b):
    return lax.dot_general(a, b, (((1,), (0,)), ((), ())), preferred_element_type=F32)


def mm_nt(a, b):
    return lax.dot_general(a, b, (((1,), (1,)), ((), ())), preferred_element_type=F32)


def mm_tn(a, b):
    return lax.dot_general(a, b, (((0,), (0,)), ((), ())), preferred_element_type=F32)


def ids(shape):
    return lax.broadcasted_iota(jnp.int32, shape, 0), lax.broadcasted_iota(jnp.int32, shape, 1)


def ones_where(mask):
    return jnp.where(mask, 1.0, 0.0).astype(BF)


def to_residue_major(seqs, rows):
    r, c = ids((seqs * rows, seqs * rows))
    return ones_where((r // seqs == c % rows) & (r % seqs == c // rows))


def normal_parts(value):
    mean = jnp.mean(value, axis=-1, keepdims=True)
    centered = value - mean
    spread = jnp.mean(centered * centered, axis=-1, keepdims=True)
    scale = lax.rsqrt(spread + 1e-05)
    return centered * scale, scale


def normal_back(cot, hat, scale):
    first = jnp.mean(cot, axis=-1, keepdims=True)
    second = jnp.mean(cot * hat, axis=-1, keepdims=True)
    return scale * (cot - first - hat * second)


def group_max(value):
    halves = []
    for h in range(2):
        x = value[:, h * 128 : (h + 1) * 128]
        lane = lax.broadcasted_iota(jnp.int32, x.shape, 1) % HEAD_DIM
        for shift in (1, 2, 4, 8, 16):
            low = pltpu.roll(x, shift, 1)
            high = pltpu.roll(x, 128 - HEAD_DIM + shift, 1)
            x = jnp.maximum(x, jnp.where(lane >= shift, low, high))
        halves.append(x)
    return jnp.concatenate(halves, axis=1)


def group_sum(value, same):
    high = value.astype(BF)
    low = (value - high.astype(F32)).astype(BF)
    return mm(high, same) + mm(low, same)


def head_mask(width):
    r, c = ids((width, width))
    return r // HEAD_DIM == c // HEAD_DIM


def spread_heads(block, mask):
    return jnp.where(mask, jnp.concatenate([block] * HEADS, axis=0), jnp.zeros((), block.dtype))


def gather_heads(value, mask):
    width = value.shape[1]
    kept = jnp.where(mask, value, 0.0)
    return jnp.sum(kept.reshape(HEADS, width // HEADS, width), axis=0)


def forward_kernel(
    where_ref, x_ref, dup_ref, seq_ref, res_ref, w_ref, aff_ref, lrt_ref,
    proj_ref, pairs_ref, nb_ref, q_ref, k_ref, v_ref, gate_ref, att_ref, p_ref, gated_ref,
    hat1_ref, rs1_ref, hat2_ref, rs2_ref, sec_ref, dup_scr, *, n,
):
    own = where_ref[0]
    seqs = seq_ref.shape[1]
    total = x_ref.shape[0]
    rows = total // seqs
    width = x_ref.shape[1]
    mask = head_mask(width)
    same = ones_where(mask)
    seq_f = seq_ref[...].astype(F32)
    res_f = res_ref[...].astype(F32)
    pair_rows = dup_ref.shape[0]
    sites = pair_rows // rows
    r, c = ids((pair_rows, pair_rows))
    swap = ones_where((r // rows == c % sites) & (r % rows == c // sites))
    dup = mm(swap, dup_ref[...])
    r, c = ids((pair_rows, sites))
    flag_j = jnp.sum(jnp.where(c == r // rows, res_f, 0.0), axis=1, keepdims=True)
    flag_i = jnp.sum(jnp.where(c == r % rows + own * rows, res_f, 0.0), axis=1, keepdims=True)
    present = jnp.sum(seq_f, axis=1, keepdims=True)
    dup_scr[...] = dup / jnp.maximum(flag_i * flag_j * present, 1.0)
    block = rows * rows
    for m in range(n):
        at = lax.rem(own + m, n) * block
        pairs_ref[m * block : (m + 1) * block, :] = dup_scr[pl.ds(pl.multiple_of(at, block), block), :].astype(BF)
    x = mm(to_residue_major(seqs, rows), x_ref[...])
    hat1, rs1 = normal_parts(x)
    hat1_ref[...] = hat1
    rs1_ref[...] = rs1
    nb = (hat1 * aff_ref[0:1, :] + aff_ref[1:2, :]).astype(BF)
    nb_ref[...] = nb
    q = (mm(nb, w_ref[0]) * HEAD_DIM ** (-0.5)).astype(BF)
    k = mm(nb, w_ref[1]).astype(BF)
    v = mm(nb, w_ref[2]).astype(BF)
    q_ref[...] = q
    k_ref[...] = k
    v_ref[...] = v
    gate = jax.nn.sigmoid(mm(nb, w_ref[3]) + aff_ref[2:3, :])
    gate_ref[...] = gate
    r, c = ids((seqs, width))
    over_t = ones_where(r == c % seqs)
    seq8 = jnp.broadcast_to(seq_f, (8, seqs)).astype(BF)
    seq_row = mm(seq8, over_t)[0:1, :]
    logits = []
    for i in range(rows):
        at = slice(i * seqs, (i + 1) * seqs)
        logits.append(mm_nt(q[at], spread_heads(k[at], mask)))
    s = jnp.concatenate(logits, axis=0) + (seq_row - 1.0) * 1000000000.0
    e = jnp.exp(s - group_max(s))
    p = e / group_sum(e, same)
    p_ref[...] = p
    pb = p.astype(BF)
    att = []
    for i in range(rows):
        at = slice(i * seqs, (i + 1) * seqs)
        att.append(mm(pb[at], spread_heads(v[at], mask)))
    att = jnp.concatenate(att, axis=0)
    att_ref[...] = att
    gated = (att * gate).astype(BF)
    gated_ref[...] = gated
    hat2, rs2 = normal_parts(x + mm(gated, w_ref[4]))
    hat2_ref[...] = hat2
    rs2_ref[...] = rs2
    sec = (hat2 * aff_ref[3:4, :] + aff_ref[4:5, :]).astype(BF)
    sec_ref[...] = sec
    proj = mm_nt(lrt_ref[...], sec)
    r, c = ids((sites, total))
    over_r = ones_where(r == c // seqs + own * rows)
    res8 = jnp.broadcast_to(res_f, (8, sites)).astype(BF)
    flags = seq_row * mm(res8, over_r)[0:1, :]
    proj_ref[...] = (proj * flags).astype(BF)


def stack_right(right_t):
    return jnp.concatenate([right_t[:, :128], right_t[:, 128:]], axis=0)


def spread_left(left_t, seqs):
    factors, total = left_t.shape
    lanes = factors * 32
    r, c = ids((factors, lanes))
    pick = ones_where(c // 32 == r)
    r, c = ids((total, lanes))
    held = jnp.where(r // seqs == c % 8, mm_tn(left_t, pick), 0.0).astype(BF)
    r, c = ids((128, total))
    out = mm(ones_where(r % seqs == c % seqs), held)
    r, c = ids((128, lanes))
    return jnp.where(r // seqs == (c // 8) % 4, out, 0.0).astype(BF)


def diagonal(panel):
    zero = jnp.zeros_like(panel)
    return jnp.concatenate(
        [jnp.concatenate([panel if b == a else zero for b in range(4)], axis=1) for a in range(4)], axis=0
    )


def pair_cotangent(wide, diag):
    d = mm_nt(wide, diag).astype(BF)
    return jnp.concatenate([d[g * 32 : (g + 1) * 32] for g in range(8)], axis=1)


def backward_kernel(
    where_ref, proj_ref, pairs_ref, other_proj_ref, other_pairs_ref, wf_ref, adj_ref, seq_ref, res_ref, w_ref, aff_ref,
    lrt_ref, nb_ref, q_ref, k_ref, v_ref, gate_ref, att_ref, p_ref, gated_ref, hat1_ref, rs1_ref,
    hat2_ref, rs2_ref, sec_ref,
    dx_ref, keep_ref, send_ref, grad_scr, *, n,
):
    own, core = where_ref[0], where_ref[1]
    seqs = seq_ref.shape[1]
    total, width = adj_ref.shape
    rows = total // seqs
    block = rows * rows
    factors = OUTER_FACTORS
    mask = head_mask(width)
    same = ones_where(mask)
    seq_f = seq_ref[...].astype(F32)
    res_f = res_ref[...].astype(F32)
    sites = res_ref.shape[1]

    wide = jnp.concatenate(
        [
            jnp.concatenate([wf_ref[g * 128 + b * 32 : g * 128 + (b + 1) * 32, :] for g in range(8)], axis=0)
            for b in range(4)
        ],
        axis=1,
    )
    rights, lefts = [], []
    for m in range(n):
        both = proj_ref[...] if m == 0 else other_proj_ref[m - 1]
        lefts.append(spread_left(both[:factors], seqs))
        rights.append(stack_right(both[factors:]))
    right = jnp.concatenate(rights, axis=0)
    diags = [diagonal(pairs_ref[g * 32 : (g + 1) * 32, :]) for g in range(2 * n)]
    cots = [pair_cotangent(wide, d) for d in diags]
    back = mm_tn(right, jnp.concatenate(cots, axis=0))
    r, c = ids(back.shape)
    back = jnp.where(r // seqs == (c // 8) % 4, back, 0.0)
    back = jnp.sum(back.reshape(4, seqs, back.shape[1]), axis=0)
    tiles = []
    for g in range(8):
        t = back[:, g * 128 : (g + 1) * 128]
        t = t + pltpu.roll(t, 8, 1)
        tiles.append(t + pltpu.roll(t, 16, 1))
    back = jnp.concatenate(tiles, axis=1).astype(BF)
    r, c = ids((total, back.shape[1]))
    back = jnp.where(c % 32 == 24 + r // seqs, jnp.concatenate([back] * rows, axis=0), jnp.zeros((), BF))
    r, c = ids((factors, back.shape[1]))
    left_cot = mm_nt(ones_where(c // 32 == r), back)
    right_cot = mm_nt(jnp.concatenate(cots[:2], axis=0), lefts[0])
    for m in range(1, n):
        inward = [
            pair_cotangent(wide, diagonal(other_pairs_ref[(m - 1) * block + g * 32 : (m - 1) * block + (g + 1) * 32, :]))
            for g in range(2)
        ]
        right_cot = right_cot + mm_nt(jnp.concatenate(inward, axis=0), lefts[m])
    right_cot = right_cot.astype(BF).astype(F32)
    right_cot = jnp.concatenate([right_cot[:factors], right_cot[factors:]], axis=1)
    outer = mm(right, lefts[0]).astype(BF)
    final = jnp.zeros((256, 512), F32)
    for g in range(2 * n):
        o = outer[g * 32 : (g + 1) * 32]
        o = jnp.concatenate([o[:, b * 128 : (b + 1) * 128] for b in range(8)], axis=0)
        final = final + mm(o, diags[g])
    base = 10 * total
    for g in range(8):
        for b in range(4):
            at = base + (4 * g + b) * 32
            grad_scr[at : at + 32, :] = final[g * 32 : (g + 1) * 32, b * 128 : (b + 1) * 128].astype(BF)

    r, c = ids((seqs, total))
    seq_row = mm(jnp.broadcast_to(seq_f, (8, seqs)).astype(BF), ones_where(r == c % seqs))[0:1, :]
    r, c = ids((sites, total))
    res_row = mm(jnp.broadcast_to(res_f, (8, sites)).astype(BF), ones_where(r == c // seqs + own * rows))[0:1, :]
    proj_cot = (jnp.concatenate([left_cot, right_cot], axis=0) * (seq_row * res_row)).astype(BF)
    base = base + 1024
    lr_grad = mm(proj_cot, sec_ref[...]).astype(BF)
    grad_scr[base : base + 64, :] = lr_grad[:, :128]
    grad_scr[base + 64 : base + 128, :] = lr_grad[:, 128:]
    base = base + 128
    turn = to_residue_major(seqs, rows)
    cot = mm_tn(proj_cot, lrt_ref[...]).astype(BF).astype(F32)
    hat2 = hat2_ref[...]
    d_gain2 = jnp.sum(cot * hat2, axis=0, keepdims=True)
    d_bias2 = jnp.sum(cot, axis=0, keepdims=True)
    upd = mm(turn, adj_ref[...]) + normal_back(cot * aff_ref[3:4, :], hat2, rs2_ref[...])

    def put(index, grad):
        grad = grad.astype(BF)
        grad_scr[2 * index * total : (2 * index + 1) * total, :] = grad[:, :128]
        grad_scr[(2 * index + 1) * total : (2 * index + 2) * total, :] = grad[:, 128:]

    upd_b = upd.astype(BF)
    d_gated = mm_nt(upd_b, w_ref[4]).astype(BF).astype(F32)
    put(4, mm_tn(gated_ref[...], upd_b))
    gate = gate_ref[...]
    d_att = d_gated * gate
    d_z = d_gated * att_ref[...] * gate * (1.0 - gate)
    d_gate_bias = jnp.sum(d_z, axis=0, keepdims=True)
    nb = nb_ref[...]
    d_zb = d_z.astype(BF)
    put(3, mm_tn(nb, d_zb))
    d_attb = d_att.astype(BF)
    p = p_ref[...]
    pb = p.astype(BF)
    d_p, d_v = [], []
    for i in range(rows):
        at = slice(i * seqs, (i + 1) * seqs)
        d_p.append(mm_nt(d_attb[at], spread_heads(v_ref[at, :], mask)))
        d_v.append(gather_heads(mm_tn(pb[at], d_attb[at]), mask))
    d_p = jnp.concatenate(d_p, axis=0).astype(BF).astype(F32)
    d_v = jnp.concatenate(d_v, axis=0).astype(BF)
    put(2, mm_tn(nb, d_v))
    d_s = (p * (d_p - group_sum(p * d_p, same))).astype(BF)
    d_q, d_k = [], []
    for i in range(rows):
        at = slice(i * seqs, (i + 1) * seqs)
        d_q.append(mm(d_s[at], spread_heads(k_ref[at, :], mask)))
        d_k.append(gather_heads(mm_tn(d_s[at], q_ref[at, :]), mask))
    d_q = jnp.concatenate(d_q, axis=0).astype(BF).astype(F32) * HEAD_DIM ** (-0.5)
    d_q = d_q.astype(BF)
    d_k = jnp.concatenate(d_k, axis=0).astype(BF)
    put(0, mm_tn(nb, d_q))
    put(1, mm_tn(nb, d_k))
    cot = mm_nt(d_q, w_ref[0]) + mm_nt(d_k, w_ref[1]) + mm_nt(d_v, w_ref[2]) + mm_nt(d_zb, w_ref[3])
    cot = cot.astype(BF).astype(F32)
    hat1 = hat1_ref[...]
    d_gain1 = jnp.sum(cot * hat1, axis=0, keepdims=True)
    d_bias1 = jnp.sum(cot, axis=0, keepdims=True)
    d_x = (upd + normal_back(cot * aff_ref[0:1, :], hat1, rs1_ref[...])).astype(BF)
    dx_ref[...] = mm_tn(turn, d_x).astype(BF)
    vectors = jnp.concatenate(
        [d_gain1, d_bias1, d_gate_bias, d_gain2, d_bias2, jnp.zeros((3, width), F32)], axis=0
    )
    grad_scr[base : base + 16, :] = jnp.concatenate([vectors[:, :128], vectors[:, 128:]], axis=0).astype(BF)
    base = base + 16
    grad_scr[base:, :] = jnp.zeros((grad_scr.shape[0] - base, 128), BF)
    half = keep_ref.shape[0]
    keep_ref[...] = grad_scr[pl.ds(pl.multiple_of(core * half, half), half), :]
    send_ref[...] = grad_scr[pl.ds(pl.multiple_of((1 - core) * half, half), half), :]


def unpack_kernel(where_ref, mine_ref, other_ref, att_ref, vec_ref, lrt_ref, final_ref, scr):
    core = where_ref[1]
    half = mine_ref.shape[0]
    scr[pl.ds(pl.multiple_of(core * half, half), half), :] = mine_ref[...]
    scr[pl.ds(pl.multiple_of((1 - core) * half, half), half), :] = other_ref[...]
    total = att_ref.shape[1]
    for w in range(5):
        for h in range(2):
            at = (2 * w + h) * total
            att_ref[w, :, h * 128 : (h + 1) * 128] = scr[at : at + total, :].astype(F32)
    base = 10 * total
    final_ref[...] = scr[base : base + 1024, :].astype(F32)
    base = base + 1024
    lrt_ref[:, :128] = scr[base : base + 64, :].astype(F32)
    lrt_ref[:, 128:] = scr[base + 64 : base + 128, :].astype(F32)
    base = base + 128
    vectors = scr[base : base + 16, :].astype(F32)
    vec_ref[:, :128] = vectors[:5]
    vec_ref[:, 128:] = vectors[8:13]


def call(kernel, outs, scratch, where, *args):
    vmem = pl.BlockSpec(memory_space=pltpu.VMEM)
    return pl.pallas_call(
        kernel,
        out_shape=[jax.ShapeDtypeStruct(s, d) for s, d in outs],
        in_specs=[pl.BlockSpec(memory_space=pltpu.SMEM)] + [vmem] * len(args),
        out_specs=[vmem] * len(outs),
        scratch_shapes=scratch,
        compiler_params=pltpu.CompilerParams(vmem_limit_bytes=48 * 1024 * 1024),
    )(where, *args)


def exchange(value, axes, total, offset):
    return lax.ppermute(value, axes, [(i, i ^ offset) for i in range(total)])


def reduce_gradients(keep, send, index, dp_size, axial_size):
    axes = ("dp", "axial")
    if axial_size != 2 or dp_size != 16:
        summed = lax.psum((keep.astype(F32), send.astype(F32)), axes)
        return summed[0].astype(BF), summed[1].astype(BF)
    total = dp_size * axial_size
    half = keep.shape[0]
    mine = keep.astype(F32) + exchange(send, axes, total, 2).astype(F32)
    place = (index % 2) + 2 * ((index // 4) % 2)
    offsets = (1, 4, 5)
    quarter = half // 4
    own = lax.dynamic_slice_in_dim(mine, place * quarter, quarter)
    got = []
    for step, offset in zip((1, 2, 3), offsets):
        piece = lax.dynamic_slice_in_dim(mine, (place ^ step) * quarter, quarter)
        got.append(exchange(piece.astype(BF), axes, total, offset))
    own = own + got[0].astype(F32) + got[1].astype(F32) + got[2].astype(F32)
    own = own.astype(BF)
    level = [exchange(own, axes, total, offset).astype(F32) for offset in (8, 16, 24)]
    own = ((own.astype(F32) + level[0]) + (level[1] + level[2])).astype(BF)
    pieces = [own] + [exchange(own, axes, total, offset) for offset in offsets]
    stacked = jnp.stack(pieces)
    mine = jnp.concatenate([lax.dynamic_index_in_dim(stacked, place ^ k, keepdims=False) for k in range(4)], axis=0)
    return mine, exchange(mine, axes, total, 2)


def per_device(
    dp_size,
    axial_size,
    homolog_activations,
    homolog_adjoint,
    duplex_adjoint,
    homolog_exists_filter,
    amino_exists_filter,
    focus_matrices_tier,
    affine_parameters,
    left_right_matrices,
    outer_final_matrix,
):
    n = axial_size
    _, seqs, rows, width = homolog_activations.shape
    total = seqs * rows
    index = lax.axis_index(("dp", "axial"))
    own = lax.axis_index("axial")
    fast = axial_size == 2 and dp_size == 16
    core = (index // 2) % 2 if fast else jnp.zeros_like(index)
    where = jnp.stack([own, core])
    x = homolog_activations.reshape(total, width)
    adj = homolog_adjoint.reshape(total, width)
    dup = duplex_adjoint.reshape(-1, DUPLEX_FEATURES)
    lrt = left_right_matrices.T
    flat_b, flat_f, column = ((total, width), BF), ((total, width), F32), ((total, 1), F32)
    block = rows * rows
    proj, pairs, *saved = call(
        partial(forward_kernel, n=n),
        [
            ((2 * OUTER_FACTORS, total), BF), ((n * block, DUPLEX_FEATURES), BF),
            flat_b, flat_b, flat_b, flat_b, flat_f, flat_f, flat_f, flat_b, flat_f, column, flat_f, column, flat_b,
        ],
        [pltpu.VMEM(dup.shape, F32)],
        where, x, dup, homolog_exists_filter, amino_exists_filter, focus_matrices_tier, affine_parameters, lrt,
    )
    other_proj, other_pairs = [], []
    for m in range(1, n):
        perm = [(a, (a - m) % n) for a in range(n)]
        at = ((n - m) % n) * block
        message = jnp.concatenate(
            [proj.reshape(-1, DUPLEX_FEATURES), pairs[at : at + block]], axis=0
        )
        message = lax.ppermute(message, "axial", perm)
        other_proj.append(message[:-block].reshape(proj.shape))
        other_pairs.append(message[-block:])
    used = 10 * total + outer_final_matrix.shape[0] + 128 + 16
    half = -(-used // 128) * 64
    dx, keep, send = call(
        partial(backward_kernel, n=n),
        [flat_b, ((half, 128), BF), ((half, 128), BF)],
        [pltpu.VMEM((2 * half, 128), BF)],
        where, proj, pairs, jnp.stack(other_proj), jnp.concatenate(other_pairs, axis=0), outer_final_matrix, adj,
        homolog_exists_filter, amino_exists_filter, focus_matrices_tier, affine_parameters, lrt, *saved,
    )
    mine, other = reduce_gradients(keep, send, index, dp_size, axial_size)
    grad_att, grad_vec, grad_lrt, grad_final = call(
        unpack_kernel,
        [
            (focus_matrices_tier.shape, F32), (affine_parameters.shape, F32), (lrt.shape, F32),
            (outer_final_matrix.shape, F32),
        ],
        [pltpu.VMEM((2 * half, 128), BF)],
        where, mine, other,
    )
    return (dx.reshape(homolog_activations.shape), grad_att, grad_vec, grad_lrt.T, grad_final)


def solution(mesh):
    return jax.shard_map(
        partial(per_device, mesh.shape["dp"], mesh.shape["axial"]),
        mesh=mesh,
        in_specs=(
            P("dp", None, "axial", None),
            P("dp", None, "axial", None),
            P("dp", "axial", None, None),
            P("dp", None),
            P("dp", None),
            P(),
            P(),
            P(),
            P(),
        ),
        out_specs=(P("dp", None, "axial", None), P(), P(), P(), P()),
        check_vma=False,
    )
```

```python
from functools import partial

import jax
import jax.numpy as jnp
from jax import lax
from jax.experimental import pallas as pl
from jax.experimental.pallas import tpu as pltpu
from jax.sharding import PartitionSpec as P

HEADS = 8
HEAD_DIM = 32
OUTER_FACTORS = 32
DUPLEX_FEATURES = 128
BF = jnp.bfloat16
F32 = jnp.float32


def mm(a, b):
    return lax.dot_general(a, b, (((1,), (0,)), ((), ())), preferred_element_type=F32)


def mm_nt(a, b):
    return lax.dot_general(a, b, (((1,), (1,)), ((), ())), preferred_element_type=F32)


def mm_tn(a, b):
    return lax.dot_general(a, b, (((0,), (0,)), ((), ())), preferred_element_type=F32)


def ids(shape):
    return lax.broadcasted_iota(jnp.int32, shape, 0), lax.broadcasted_iota(jnp.int32, shape, 1)


def ones_where(mask):
    return jnp.where(mask, 1.0, 0.0).astype(BF)


def to_residue_major(seqs, rows):
    r, c = ids((seqs * rows, seqs * rows))
    return ones_where((r // seqs == c % rows) & (r % seqs == c // rows))


def normal_parts(value):
    mean = jnp.mean(value, axis=-1, keepdims=True)
    centered = value - mean
    spread = jnp.mean(centered * centered, axis=-1, keepdims=True)
    scale = lax.rsqrt(spread + 1e-05)
    return centered * scale, scale


def normal_back(cot, hat, scale):
    first = jnp.mean(cot, axis=-1, keepdims=True)
    second = jnp.mean(cot * hat, axis=-1, keepdims=True)
    return scale * (cot - first - hat * second)


def group_max(value):
    halves = []
    for h in range(2):
        x = value[:, h * 128 : (h + 1) * 128]
        lane = lax.broadcasted_iota(jnp.int32, x.shape, 1) % HEAD_DIM
        for shift in (1, 2, 4, 8, 16):
            low = pltpu.roll(x, shift, 1)
            high = pltpu.roll(x, 128 - HEAD_DIM + shift, 1)
            x = jnp.maximum(x, jnp.where(lane >= shift, low, high))
        halves.append(x)
    return jnp.concatenate(halves, axis=1)


def group_sum(value, same):
    high = value.astype(BF)
    low = (value - high.astype(F32)).astype(BF)
    return mm(high, same) + mm(low, same)


def head_mask(width):
    r, c = ids((width, width))
    return r // HEAD_DIM == c // HEAD_DIM


def spread_heads(block, mask):
    return jnp.where(mask, jnp.concatenate([block] * HEADS, axis=0), jnp.zeros((), block.dtype))


def gather_heads(value, mask):
    width = value.shape[1]
    kept = jnp.where(mask, value, 0.0)
    return jnp.sum(kept.reshape(HEADS, width // HEADS, width), axis=0)


def forward_kernel(
    where_ref, x_hbm, dup_hbm, seq_hbm, res_hbm, w_hbm, aff_hbm, lrt_hbm, wf_hbm, adj_hbm,
    proj_ref, pairs_ref, nb_ref, q_ref, k_ref, v_ref, gate_ref, att_ref, p_ref, gated_ref,
    hat1_ref, rs1_ref, hat2_ref, rs2_ref, sec_ref, out_ref,
    seq_ref, res_ref, w_ref, aff_ref, lrt_ref, wf_ref, adj_ref,
    x_ref, dup_ref, dup_scr, sems, *, n,
):
    own = where_ref[0]
    pairs_of = [
        (x_hbm, x_ref), (aff_hbm, aff_ref), (seq_hbm, seq_ref), (res_hbm, res_ref), (dup_hbm, dup_ref),
        (w_hbm, w_ref), (lrt_hbm, lrt_ref), (wf_hbm, wf_ref), (adj_hbm, adj_ref),
    ]
    copies = [pltpu.make_async_copy(src, dst, sems.at[i]) for i, (src, dst) in enumerate(pairs_of)]
    for copy in copies:
        copy.start()
    for copy in copies[:5]:
        copy.wait()
    seqs = seq_ref.shape[1]
    total = x_ref.shape[0]
    rows = total // seqs
    width = x_ref.shape[1]
    mask = head_mask(width)
    same = ones_where(mask)
    seq_f = seq_ref[...].astype(F32)
    res_f = res_ref[...].astype(F32)
    pair_rows = dup_ref.shape[0]
    sites = pair_rows // rows
    r, c = ids((pair_rows, pair_rows))
    swap = ones_where((r // rows == c % sites) & (r % rows == c // sites))
    dup = mm(swap, dup_ref[...])
    r, c = ids((pair_rows, sites))
    flag_j = jnp.sum(jnp.where(c == r // rows, res_f, 0.0), axis=1, keepdims=True)
    flag_i = jnp.sum(jnp.where(c == r % rows + own * rows, res_f, 0.0), axis=1, keepdims=True)
    present = jnp.sum(seq_f, axis=1, keepdims=True)
    dup_scr[...] = dup / jnp.maximum(flag_i * flag_j * present, 1.0)
    block = rows * rows
    for m in range(n):
        at = lax.rem(own + m, n) * block
        piece = dup_scr[pl.ds(pl.multiple_of(at, block), block), :].astype(BF)
        pairs_ref[m * block : (m + 1) * block, :] = piece
        if m > 0:
            out_ref[n - 1 - m, 128:, :] = piece
    x = mm(to_residue_major(seqs, rows), x_ref[...])
    hat1, rs1 = normal_parts(x)
    hat1_ref[...] = hat1
    rs1_ref[...] = rs1
    nb = (hat1 * aff_ref[0:1, :] + aff_ref[1:2, :]).astype(BF)
    nb_ref[...] = nb
    copies[5].wait()
    q = (mm(nb, w_ref[0]) * HEAD_DIM ** (-0.5)).astype(BF)
    k = mm(nb, w_ref[1]).astype(BF)
    v = mm(nb, w_ref[2]).astype(BF)
    q_ref[...] = q
    k_ref[...] = k
    v_ref[...] = v
    gate = jax.nn.sigmoid(mm(nb, w_ref[3]) + aff_ref[2:3, :])
    gate_ref[...] = gate
    r, c = ids((seqs, width))
    over_t = ones_where(r == c % seqs)
    seq8 = jnp.broadcast_to(seq_f, (8, seqs)).astype(BF)
    seq_row = mm(seq8, over_t)[0:1, :]
    logits = []
    for i in range(rows):
        at = slice(i * seqs, (i + 1) * seqs)
        logits.append(mm_nt(q[at], spread_heads(k[at], mask)))
    s = jnp.concatenate(logits, axis=0) + (seq_row - 1.0) * 1000000000.0
    e = jnp.exp(s - group_max(s))
    p = e / group_sum(e, same)
    p_ref[...] = p
    pb = p.astype(BF)
    att = []
    for i in range(rows):
        at = slice(i * seqs, (i + 1) * seqs)
        att.append(mm(pb[at], spread_heads(v[at], mask)))
    att = jnp.concatenate(att, axis=0)
    att_ref[...] = att
    gated = (att * gate).astype(BF)
    gated_ref[...] = gated
    hat2, rs2 = normal_parts(x + mm(gated, w_ref[4]))
    hat2_ref[...] = hat2
    rs2_ref[...] = rs2
    sec = (hat2 * aff_ref[3:4, :] + aff_ref[4:5, :]).astype(BF)
    sec_ref[...] = sec
    for copy in copies[6:]:
        copy.wait()
    proj = mm_nt(lrt_ref[...], sec)
    r, c = ids((sites, total))
    over_r = ones_where(r == c // seqs + own * rows)
    res8 = jnp.broadcast_to(res_f, (8, sites)).astype(BF)
    flags = seq_row * mm(res8, over_r)[0:1, :]
    proj = (proj * flags).astype(BF)
    proj_ref[...] = proj
    for m in range(n - 1):
        out_ref[m, :64, :] = proj[:, :128]
        out_ref[m, 64:128, :] = proj[:, 128:]


def stack_right(right_t):
    return jnp.concatenate([right_t[:, :128], right_t[:, 128:]], axis=0)


def spread_left(left_t, seqs):
    factors, total = left_t.shape
    lanes = factors * 32
    r, c = ids((factors, lanes))
    pick = ones_where(c // 32 == r)
    r, c = ids((total, lanes))
    held = jnp.where(r // seqs == c % 8, mm_tn(left_t, pick), 0.0).astype(BF)
    r, c = ids((128, total))
    out = mm(ones_where(r % seqs == c % seqs), held)
    r, c = ids((128, lanes))
    return jnp.where(r // seqs == (c // 8) % 4, out, 0.0).astype(BF)


def diagonal(panel):
    zero = jnp.zeros_like(panel)
    return jnp.concatenate(
        [jnp.concatenate([panel if b == a else zero for b in range(4)], axis=1) for a in range(4)], axis=0
    )


def pair_cotangent(wide, diag):
    d = mm_nt(wide, diag).astype(BF)
    return jnp.concatenate([d[g * 32 : (g + 1) * 32] for g in range(8)], axis=1)


def sum_groups(value, seqs):
    r, c = ids(value.shape)
    kept = jnp.where(r // seqs == (c // 8) % 4, value, 0.0)
    return jnp.sum(kept.reshape(4, seqs, value.shape[1]), axis=0)


def outer_groups(outer, g):
    o = outer[g * 32 : (g + 1) * 32]
    return jnp.concatenate([o[:, b * 128 : (b + 1) * 128] for b in range(8)], axis=0)


def widen(wf_ref):
    return jnp.concatenate(
        [
            jnp.concatenate([wf_ref[g * 128 + b * 32 : g * 128 + (b + 1) * 32, :] for g in range(8)], axis=0)
            for b in range(4)
        ],
        axis=1,
    )


def local_pairs_kernel(
    proj_ref, pairs_ref, wf_ref, seq_ref, adj_ref,
    cots_ref, left_ref, back_ref, right_cot_ref, final_ref, wide_ref, adj_out_ref, *, n,
):
    seqs = seq_ref.shape[1]
    total = adj_ref.shape[0]
    factors = OUTER_FACTORS
    wide = widen(wf_ref)
    wide_ref[...] = wide
    both = proj_ref[...]
    left = spread_left(both[:factors], seqs)
    left_ref[...] = left
    right = stack_right(both[factors:])
    diags = [diagonal(pairs_ref[g * 32 : (g + 1) * 32, :]) for g in range(2 * n)]
    cots = [pair_cotangent(wide, d) for d in diags]
    for g in range(2 * n):
        cots_ref[g * 32 : (g + 1) * 32, :] = cots[g]
    near = jnp.concatenate(cots[:2], axis=0)
    back_ref[...] = sum_groups(mm_tn(right, near), seqs)
    right_cot_ref[...] = mm_nt(near, left)
    outer = mm(right, left).astype(BF)
    final_ref[...] = mm(outer_groups(outer, 0), diags[0]) + mm(outer_groups(outer, 1), diags[1])
    adj_out_ref[...] = mm(to_residue_major(seqs, total // seqs), adj_ref[...])


def backward_kernel(
    where_ref, other_ref, pairs_ref, cots_ref, left_ref, back_ref, right_cot_ref, final_ref, wide_ref, adj_ref,
    seq_ref, res_ref, w_ref, aff_ref,
    lrt_ref, nb_ref, q_ref, k_ref, v_ref, gate_ref, att_ref, p_ref, gated_ref, hat1_ref, rs1_ref,
    hat2_ref, rs2_ref, sec_ref,
    dx_ref, keep_ref, send_ref, grad_scr, *, n,
):
    own, core = where_ref[0], where_ref[1]
    seqs = seq_ref.shape[1]
    total, width = adj_ref.shape
    rows = total // seqs
    block = rows * rows
    factors = OUTER_FACTORS
    mask = head_mask(width)
    same = ones_where(mask)
    seq_f = seq_ref[...].astype(F32)
    res_f = res_ref[...].astype(F32)
    sites = res_ref.shape[1]

    wide = wide_ref[...]
    rights = []
    right_cot = right_cot_ref[...]
    for m in range(1, n):
        both = jnp.concatenate([other_ref[m - 1, :64, :], other_ref[m - 1, 64:128, :]], axis=1)
        rights.append(stack_right(both[factors:]))
        inward = [pair_cotangent(wide, diagonal(other_ref[m - 1, 128 + g * 32 : 160 + g * 32, :])) for g in range(2)]
        right_cot = right_cot + mm_nt(jnp.concatenate(inward, axis=0), spread_left(both[:factors], seqs))
    right = jnp.concatenate(rights, axis=0)
    back = back_ref[...] + sum_groups(mm_tn(right, cots_ref[block:, :]), seqs)
    tiles = []
    for g in range(8):
        t = back[:, g * 128 : (g + 1) * 128]
        t = t + pltpu.roll(t, 8, 1)
        tiles.append(t + pltpu.roll(t, 16, 1))
    back = jnp.concatenate(tiles, axis=1).astype(BF)
    r, c = ids((total, back.shape[1]))
    back = jnp.where(c % 32 == 24 + r // seqs, jnp.concatenate([back] * rows, axis=0), jnp.zeros((), BF))
    r, c = ids((factors, back.shape[1]))
    left_cot = mm_nt(ones_where(c // 32 == r), back)
    right_cot = right_cot.astype(BF).astype(F32)
    right_cot = jnp.concatenate([right_cot[:factors], right_cot[factors:]], axis=1)
    outer = mm(right, left_ref[...]).astype(BF)
    final = final_ref[...]
    for g in range(2 * (n - 1)):
        final = final + mm(outer_groups(outer, g), diagonal(pairs_ref[block + g * 32 : block + (g + 1) * 32, :]))
    base = 10 * total
    for g in range(8):
        for b in range(4):
            at = base + (4 * g + b) * 32
            grad_scr[at : at + 32, :] = final[g * 32 : (g + 1) * 32, b * 128 : (b + 1) * 128].astype(BF)

    r, c = ids((seqs, total))
    seq_row = mm(jnp.broadcast_to(seq_f, (8, seqs)).astype(BF), ones_where(r == c % seqs))[0:1, :]
    r, c = ids((sites, total))
    res_row = mm(jnp.broadcast_to(res_f, (8, sites)).astype(BF), ones_where(r == c // seqs + own * rows))[0:1, :]
    proj_cot = (jnp.concatenate([left_cot, right_cot], axis=0) * (seq_row * res_row)).astype(BF)
    base = base + 1024
    lr_grad = mm(proj_cot, sec_ref[...]).astype(BF)
    grad_scr[base : base + 64, :] = lr_grad[:, :128]
    grad_scr[base + 64 : base + 128, :] = lr_grad[:, 128:]
    base = base + 128
    cot = mm_tn(proj_cot, lrt_ref[...]).astype(BF).astype(F32)
    hat2 = hat2_ref[...]
    d_gain2 = jnp.sum(cot * hat2, axis=0, keepdims=True)
    d_bias2 = jnp.sum(cot, axis=0, keepdims=True)
    upd = adj_ref[...] + normal_back(cot * aff_ref[3:4, :], hat2, rs2_ref[...])

    def put(index, grad):
        grad = grad.astype(BF)
        grad_scr[2 * index * total : (2 * index + 1) * total, :] = grad[:, :128]
        grad_scr[(2 * index + 1) * total : (2 * index + 2) * total, :] = grad[:, 128:]

    upd_b = upd.astype(BF)
    d_gated = mm_nt(upd_b, w_ref[4]).astype(BF).astype(F32)
    put(4, mm_tn(gated_ref[...], upd_b))
    gate = gate_ref[...]
    d_att = d_gated * gate
    d_z = d_gated * att_ref[...] * gate * (1.0 - gate)
    d_gate_bias = jnp.sum(d_z, axis=0, keepdims=True)
    nb = nb_ref[...]
    d_zb = d_z.astype(BF)
    put(3, mm_tn(nb, d_zb))
    d_attb = d_att.astype(BF)
    p = p_ref[...]
    pb = p.astype(BF)
    d_p, d_v = [], []
    for i in range(rows):
        at = slice(i * seqs, (i + 1) * seqs)
        d_p.append(mm_nt(d_attb[at], spread_heads(v_ref[at, :], mask)))
        d_v.append(gather_heads(mm_tn(pb[at], d_attb[at]), mask))
    d_p = jnp.concatenate(d_p, axis=0).astype(BF).astype(F32)
    d_v = jnp.concatenate(d_v, axis=0).astype(BF)
    put(2, mm_tn(nb, d_v))
    d_s = (p * (d_p - group_sum(p * d_p, same))).astype(BF)
    d_q, d_k = [], []
    for i in range(rows):
        at = slice(i * seqs, (i + 1) * seqs)
        d_q.append(mm(d_s[at], spread_heads(k_ref[at, :], mask)))
        d_k.append(gather_heads(mm_tn(d_s[at], q_ref[at, :]), mask))
    d_q = jnp.concatenate(d_q, axis=0).astype(BF).astype(F32) * HEAD_DIM ** (-0.5)
    d_q = d_q.astype(BF)
    d_k = jnp.concatenate(d_k, axis=0).astype(BF)
    put(0, mm_tn(nb, d_q))
    put(1, mm_tn(nb, d_k))
    cot = mm_nt(d_q, w_ref[0]) + mm_nt(d_k, w_ref[1]) + mm_nt(d_v, w_ref[2]) + mm_nt(d_zb, w_ref[3])
    cot = cot.astype(BF).astype(F32)
    hat1 = hat1_ref[...]
    d_gain1 = jnp.sum(cot * hat1, axis=0, keepdims=True)
    d_bias1 = jnp.sum(cot, axis=0, keepdims=True)
    d_x = (upd + normal_back(cot * aff_ref[0:1, :], hat1, rs1_ref[...])).astype(BF)
    dx_ref[...] = mm_tn(to_residue_major(seqs, rows), d_x).astype(BF)
    vectors = jnp.concatenate(
        [d_gain1, d_bias1, d_gate_bias, d_gain2, d_bias2, jnp.zeros((3, width), F32)], axis=0
    )
    grad_scr[base : base + 16, :] = jnp.concatenate([vectors[:, :128], vectors[:, 128:]], axis=0).astype(BF)
    base = base + 16
    grad_scr[base:, :] = jnp.zeros((grad_scr.shape[0] - base, 128), BF)
    half = keep_ref.shape[0]
    keep_ref[...] = grad_scr[pl.ds(pl.multiple_of(core * half, half), half), :]
    send_ref[...] = grad_scr[pl.ds(pl.multiple_of((1 - core) * half, half), half), :]


def unpack_kernel(where_ref, mine_ref, other_ref, att_ref, vec_ref, lrt_ref, final_ref, scr):
    core = where_ref[1]
    half = mine_ref.shape[0]
    scr[pl.ds(pl.multiple_of(core * half, half), half), :] = mine_ref[...]
    scr[pl.ds(pl.multiple_of((1 - core) * half, half), half), :] = other_ref[...]
    total = att_ref.shape[1]
    for w in range(5):
        for h in range(2):
            at = (2 * w + h) * total
            att_ref[w, :, h * 128 : (h + 1) * 128] = scr[at : at + total, :].astype(F32)
    base = 10 * total
    final_ref[...] = scr[base : base + 1024, :].astype(F32)
    base = base + 1024
    lrt_ref[:, :128] = scr[base : base + 64, :].astype(F32)
    lrt_ref[:, 128:] = scr[base + 64 : base + 128, :].astype(F32)
    base = base + 128
    vectors = scr[base : base + 16, :].astype(F32)
    vec_ref[:, :128] = vectors[:5]
    vec_ref[:, 128:] = vectors[8:13]


def call(kernel, outs, scratch, where, *args, space=pltpu.VMEM):
    return pl.pallas_call(
        kernel,
        out_shape=[jax.ShapeDtypeStruct(s, d) for s, d in outs],
        in_specs=[pl.BlockSpec(memory_space=pltpu.SMEM)] * len(where) + [pl.BlockSpec(memory_space=space)] * len(args),
        out_specs=[pl.BlockSpec(memory_space=pltpu.VMEM)] * len(outs),
        scratch_shapes=scratch,
        compiler_params=pltpu.CompilerParams(vmem_limit_bytes=24 * 1024 * 1024),
    )(*where, *[pltpu.with_memory_space_constraint(a, space) for a in args] if space != pltpu.VMEM else args)


def exchange(value, axes, total, offset):
    return lax.ppermute(value, axes, [(i, i ^ offset) for i in range(total)])


def reduce_gradients(keep, send, index, dp_size, axial_size):
    axes = ("dp", "axial")
    if axial_size != 2 or dp_size != 16:
        summed = lax.psum((keep.astype(F32), send.astype(F32)), axes)
        return summed[0].astype(BF), summed[1].astype(BF)
    total = dp_size * axial_size
    half = keep.shape[0]
    mine = keep.astype(F32) + exchange(send, axes, total, 2).astype(F32)
    place = (index % 2) + 2 * ((index // 4) % 2)
    offsets = (1, 4, 5)
    quarter = half // 4
    own = lax.dynamic_slice_in_dim(mine, place * quarter, quarter)
    got = []
    for step, offset in zip((1, 2, 3), offsets):
        piece = lax.dynamic_slice_in_dim(mine, (place ^ step) * quarter, quarter)
        got.append(exchange(piece.astype(BF), axes, total, offset))
    own = own + got[0].astype(F32) + got[1].astype(F32) + got[2].astype(F32)
    own = own.astype(BF)
    level = [exchange(own, axes, total, offset).astype(F32) for offset in (8, 16, 24)]
    own = ((own.astype(F32) + level[0]) + (level[1] + level[2])).astype(BF)
    pieces = [own] + [exchange(own, axes, total, offset) for offset in offsets]
    stacked = jnp.stack(pieces)
    mine = jnp.concatenate([lax.dynamic_index_in_dim(stacked, place ^ k, keepdims=False) for k in range(4)], axis=0)
    return mine, exchange(mine, axes, total, 2)


def per_device(
    dp_size,
    axial_size,
    homolog_activations,
    homolog_adjoint,
    duplex_adjoint,
    homolog_exists_filter,
    amino_exists_filter,
    focus_matrices_tier,
    affine_parameters,
    left_right_matrices,
    outer_final_matrix,
):
    n = axial_size
    _, seqs, rows, width = homolog_activations.shape
    total = seqs * rows
    index = lax.axis_index(("dp", "axial"))
    own = lax.axis_index("axial")
    fast = axial_size == 2 and dp_size == 16
    core = (index // 2) % 2 if fast else jnp.zeros_like(index)
    where = [jnp.stack([own, core])]
    x = homolog_activations.reshape(total, width)
    adj = homolog_adjoint.reshape(total, width)
    dup = duplex_adjoint.reshape(-1, DUPLEX_FEATURES)
    lrt = left_right_matrices.T
    flat_b, flat_f, column = ((total, width), BF), ((total, width), F32), ((total, 1), F32)
    block = rows * rows
    lanes = OUTER_FACTORS * 32
    inputs = (homolog_exists_filter, amino_exists_filter, focus_matrices_tier, affine_parameters, lrt, outer_final_matrix)
    results = call(
        partial(forward_kernel, n=n),
        [
            ((2 * OUTER_FACTORS, total), BF), ((n * block, DUPLEX_FEATURES), BF),
            flat_b, flat_b, flat_b, flat_b, flat_f, flat_f, flat_f, flat_b, flat_f, column, flat_f, column, flat_b,
            ((n - 1, 128 + block, DUPLEX_FEATURES), BF),
        ] + [(a.shape, a.dtype) for a in (*inputs, adj)],
        [pltpu.VMEM(x.shape, BF), pltpu.VMEM(dup.shape, BF), pltpu.VMEM(dup.shape, F32), pltpu.SemaphoreType.DMA((9,))],
        where, x, dup, *inputs, adj, space=pltpu.HBM,
    )
    proj, pairs, saved, messages = results[0], results[1], results[2:15], results[15]
    seq, res, w, aff, lrt, wf, adj = results[16:]
    others = [lax.ppermute(messages[m - 1], "axial", [(a, (a - m) % n) for a in range(n)]) for m in range(1, n)]
    near = call(
        partial(local_pairs_kernel, n=n),
        [
            ((n * block, lanes), BF), ((128, lanes), BF), ((seqs, lanes), F32), ((block, 128), F32), ((256, 512), F32),
            ((256, 512), BF), flat_f,
        ],
        [],
        [], proj, pairs, wf, seq, adj,
    )
    used = 10 * total + outer_final_matrix.shape[0] + 128 + 16
    half = -(-used // 128) * 64
    dx, keep, send = call(
        partial(backward_kernel, n=n),
        [flat_b, ((half, 128), BF), ((half, 128), BF)],
        [pltpu.VMEM((2 * half, 128), BF)],
        where, jnp.stack(others), pairs, *near, seq, res, w, aff, lrt, *saved,
    )
    mine, other = reduce_gradients(keep, send, index, dp_size, axial_size)
    grad_att, grad_vec, grad_lrt, grad_final = call(
        unpack_kernel,
        [
            (focus_matrices_tier.shape, F32), (affine_parameters.shape, F32), (lrt.shape, F32),
            (outer_final_matrix.shape, F32),
        ],
        [pltpu.VMEM((2 * half, 128), BF)],
        where, mine, other,
    )
    return (dx.reshape(homolog_activations.shape), grad_att, grad_vec, grad_lrt.T, grad_final)


def solution(mesh):
    return jax.shard_map(
        partial(per_device, mesh.shape["dp"], mesh.shape["axial"]),
        mesh=mesh,
        in_specs=(
            P("dp", None, "axial", None),
            P("dp", None, "axial", None),
            P("dp", "axial", None, None),
            P("dp", None),
            P("dp", None),
            P(),
            P(),
            P(),
            P(),
        ),
        out_specs=(P("dp", None, "axial", None), P(), P(), P(), P()),
        check_vma=False,
    )
```

```python
from functools import partial

import jax
import jax.numpy as jnp
from jax import lax
from jax.experimental import pallas as pl
from jax.experimental.pallas import tpu as pltpu
from jax.sharding import PartitionSpec as P

HEADS = 8
HEAD_DIM = 32
OUTER_FACTORS = 32
DUPLEX_FEATURES = 128
BF = jnp.bfloat16
F32 = jnp.float32


def mm(a, b):
    return lax.dot_general(a, b, (((1,), (0,)), ((), ())), preferred_element_type=F32)


def mm_nt(a, b):
    return lax.dot_general(a, b, (((1,), (1,)), ((), ())), preferred_element_type=F32)


def mm_tn(a, b):
    return lax.dot_general(a, b, (((0,), (0,)), ((), ())), preferred_element_type=F32)


def ids(shape):
    return lax.broadcasted_iota(jnp.int32, shape, 0), lax.broadcasted_iota(jnp.int32, shape, 1)


def ones_where(mask):
    return jnp.where(mask, 1.0, 0.0).astype(BF)


def to_residue_major(seqs, rows):
    r, c = ids((seqs * rows, seqs * rows))
    return ones_where((r // seqs == c % rows) & (r % seqs == c // rows))


def normal_parts(value):
    mean = jnp.mean(value, axis=-1, keepdims=True)
    centered = value - mean
    spread = jnp.mean(centered * centered, axis=-1, keepdims=True)
    scale = lax.rsqrt(spread + 1e-05)
    return centered * scale, scale


def normal_back(cot, hat, scale):
    first = jnp.mean(cot, axis=-1, keepdims=True)
    second = jnp.mean(cot * hat, axis=-1, keepdims=True)
    return scale * (cot - first - hat * second)


def group_max(value):
    halves = []
    for h in range(2):
        x = value[:, h * 128 : (h + 1) * 128]
        lane = lax.broadcasted_iota(jnp.int32, x.shape, 1) % HEAD_DIM
        for shift in (1, 2, 4, 8, 16):
            low = pltpu.roll(x, shift, 1)
            high = pltpu.roll(x, 128 - HEAD_DIM + shift, 1)
            x = jnp.maximum(x, jnp.where(lane >= shift, low, high))
        halves.append(x)
    return jnp.concatenate(halves, axis=1)


def group_sum(value, same):
    high = value.astype(BF)
    low = (value - high.astype(F32)).astype(BF)
    return mm(high, same) + mm(low, same)


def head_mask(width):
    r, c = ids((width, width))
    return r // HEAD_DIM == c // HEAD_DIM


def spread_heads(block, mask):
    return jnp.where(mask, jnp.concatenate([block] * HEADS, axis=0), jnp.zeros((), block.dtype))


def gather_heads(value, mask):
    width = value.shape[1]
    kept = jnp.where(mask, value, 0.0)
    return jnp.sum(kept.reshape(HEADS, width // HEADS, width), axis=0)


def forward_kernel(
    where_ref, x_hbm, dup_hbm, seq_hbm, res_hbm, w_hbm, aff_hbm, lrt_hbm, wf_hbm, adj_hbm,
    proj_ref, pairs_ref, nb_ref, q_ref, k_ref, v_ref, gate_ref, att_ref, p_ref, gated_ref,
    hat1_ref, rs1_ref, hat2_ref, rs2_ref, sec_ref, out_ref,
    seq_ref, res_ref, w_ref, aff_ref, lrt_ref, wf_ref, adj_ref,
    x_ref, dup_ref, dup_scr, sems, *, n,
):
    own = where_ref[0]
    pairs_of = [
        (x_hbm, x_ref), (aff_hbm, aff_ref), (seq_hbm, seq_ref), (res_hbm, res_ref), (dup_hbm, dup_ref),
        (w_hbm, w_ref), (lrt_hbm, lrt_ref), (wf_hbm, wf_ref), (adj_hbm, adj_ref),
    ]
    copies = [pltpu.make_async_copy(src, dst, sems.at[i]) for i, (src, dst) in enumerate(pairs_of)]
    for copy in copies:
        copy.start()
    for copy in copies[:5]:
        copy.wait()
    seqs = seq_ref.shape[1]
    total = x_ref.shape[0]
    rows = total // seqs
    width = x_ref.shape[1]
    mask = head_mask(width)
    same = ones_where(mask)
    seq_f = seq_ref[...].astype(F32)
    res_f = res_ref[...].astype(F32)
    pair_rows = dup_ref.shape[0]
    sites = pair_rows // rows
    r, c = ids((pair_rows, pair_rows))
    swap = ones_where((r // rows == c % sites) & (r % rows == c // sites))
    dup = mm(swap, dup_ref[...])
    r, c = ids((pair_rows, sites))
    flag_j = jnp.sum(jnp.where(c == r // rows, res_f, 0.0), axis=1, keepdims=True)
    flag_i = jnp.sum(jnp.where(c == r % rows + own * rows, res_f, 0.0), axis=1, keepdims=True)
    present = jnp.sum(seq_f, axis=1, keepdims=True)
    dup_scr[...] = dup / jnp.maximum(flag_i * flag_j * present, 1.0)
    block = rows * rows
    for m in range(n):
        at = lax.rem(own + m, n) * block
        piece = dup_scr[pl.ds(pl.multiple_of(at, block), block), :].astype(BF)
        pairs_ref[m * block : (m + 1) * block, :] = piece
        if m > 0:
            out_ref[n - 1 - m, 128:, :] = piece
    x = mm(to_residue_major(seqs, rows), x_ref[...])
    hat1, rs1 = normal_parts(x)
    hat1_ref[...] = hat1
    rs1_ref[...] = rs1
    nb = (hat1 * aff_ref[0:1, :] + aff_ref[1:2, :]).astype(BF)
    nb_ref[...] = nb
    copies[5].wait()
    q = (mm(nb, w_ref[0]) * HEAD_DIM ** (-0.5)).astype(BF)
    k = mm(nb, w_ref[1]).astype(BF)
    v = mm(nb, w_ref[2]).astype(BF)
    q_ref[...] = q
    k_ref[...] = k
    v_ref[...] = v
    gate = jax.nn.sigmoid(mm(nb, w_ref[3]) + aff_ref[2:3, :])
    gate_ref[...] = gate
    r, c = ids((seqs, width))
    over_t = ones_where(r == c % seqs)
    seq8 = jnp.broadcast_to(seq_f, (8, seqs)).astype(BF)
    seq_row = mm(seq8, over_t)[0:1, :]
    logits = []
    for i in range(rows):
        at = slice(i * seqs, (i + 1) * seqs)
        logits.append(mm_nt(q[at], spread_heads(k[at], mask)))
    s = jnp.concatenate(logits, axis=0) + (seq_row - 1.0) * 1000000000.0
    e = jnp.exp(s - group_max(s))
    p = e / group_sum(e, same)
    p_ref[...] = p
    pb = p.astype(BF)
    att = []
    for i in range(rows):
        at = slice(i * seqs, (i + 1) * seqs)
        att.append(mm(pb[at], spread_heads(v[at], mask)))
    att = jnp.concatenate(att, axis=0)
    att_ref[...] = att
    gated = (att * gate).astype(BF)
    gated_ref[...] = gated
    hat2, rs2 = normal_parts(x + mm(gated, w_ref[4]))
    hat2_ref[...] = hat2
    rs2_ref[...] = rs2
    sec = (hat2 * aff_ref[3:4, :] + aff_ref[4:5, :]).astype(BF)
    sec_ref[...] = sec
    for copy in copies[6:]:
        copy.wait()
    proj = mm_nt(lrt_ref[...], sec)
    r, c = ids((sites, total))
    over_r = ones_where(r == c // seqs + own * rows)
    res8 = jnp.broadcast_to(res_f, (8, sites)).astype(BF)
    flags = seq_row * mm(res8, over_r)[0:1, :]
    proj = (proj * flags).astype(BF)
    proj_ref[...] = proj
    for m in range(n - 1):
        out_ref[m, :64, :] = proj[:, :128]
        out_ref[m, 64:128, :] = proj[:, 128:]


def stack_right(right_t):
    return jnp.concatenate([right_t[:, :128], right_t[:, 128:]], axis=0)


def spread_left(left_t, seqs):
    factors, total = left_t.shape
    lanes = factors * 32
    r, c = ids((factors, lanes))
    pick = ones_where(c // 32 == r)
    r, c = ids((total, lanes))
    held = jnp.where(r // seqs == c % 8, mm_tn(left_t, pick), 0.0).astype(BF)
    r, c = ids((128, total))
    out = mm(ones_where(r % seqs == c % seqs), held)
    r, c = ids((128, lanes))
    return jnp.where(r // seqs == (c // 8) % 4, out, 0.0).astype(BF)


def diagonal(panel):
    zero = jnp.zeros_like(panel)
    return jnp.concatenate(
        [jnp.concatenate([panel if b == a else zero for b in range(4)], axis=1) for a in range(4)], axis=0
    )


def pair_cotangent(wide, diag):
    d = mm_nt(wide, diag).astype(BF)
    return jnp.concatenate([d[g * 32 : (g + 1) * 32] for g in range(8)], axis=1)


def sum_groups(value, seqs):
    r, c = ids(value.shape)
    kept = jnp.where(r // seqs == (c // 8) % 4, value, 0.0)
    return jnp.sum(kept.reshape(4, seqs, value.shape[1]), axis=0)


def outer_groups(outer, g):
    o = outer[g * 32 : (g + 1) * 32]
    return jnp.concatenate([o[:, b * 128 : (b + 1) * 128] for b in range(8)], axis=0)


def widen(wf_ref):
    return jnp.concatenate(
        [
            jnp.concatenate([wf_ref[g * 128 + b * 32 : g * 128 + (b + 1) * 32, :] for g in range(8)], axis=0)
            for b in range(4)
        ],
        axis=1,
    )


def local_pairs_kernel(
    proj_ref, pairs_ref, wf_ref, seq_ref, adj_ref,
    cots_ref, left_ref, back_ref, right_cot_ref, final_ref, wide_ref, adj_out_ref, *, n,
):
    seqs = seq_ref.shape[1]
    total = adj_ref.shape[0]
    factors = OUTER_FACTORS
    wide = widen(wf_ref)
    wide_ref[...] = wide
    both = proj_ref[...]
    left = spread_left(both[:factors], seqs)
    left_ref[...] = left
    right = stack_right(both[factors:])
    diags = [diagonal(pairs_ref[g * 32 : (g + 1) * 32, :]) for g in range(2 * n)]
    cots = [pair_cotangent(wide, d) for d in diags]
    for g in range(2 * n):
        cots_ref[g * 32 : (g + 1) * 32, :] = cots[g]
    near = jnp.concatenate(cots[:2], axis=0)
    back_ref[...] = sum_groups(mm_tn(right, near), seqs)
    right_cot_ref[...] = mm_nt(near, left)
    outer = mm(right, left).astype(BF)
    final_ref[...] = mm(outer_groups(outer, 0), diags[0]) + mm(outer_groups(outer, 1), diags[1])
    adj_out_ref[...] = mm(to_residue_major(seqs, total // seqs), adj_ref[...])


def split_halves(core, keep_ref, send_ref, grad_scr):
    half = keep_ref.shape[0]
    keep_ref[...] = grad_scr[pl.ds(pl.multiple_of(core * half, half), half), :]
    send_ref[...] = grad_scr[pl.ds(pl.multiple_of((1 - core) * half, half), half), :]


def pairs_kernel(
    where_ref, other_ref, pairs_ref, cots_ref, left_ref, back_ref, right_cot_ref, final_ref, wide_ref,
    seq_ref, res_ref, sec_ref,
    proj_cot_ref, keep_ref, send_ref, grad_scr, *, n,
):
    own, core = where_ref[0], where_ref[1]
    seqs = seq_ref.shape[1]
    total = sec_ref.shape[0]
    rows = total // seqs
    block = rows * rows
    factors = OUTER_FACTORS
    seq_f = seq_ref[...].astype(F32)
    res_f = res_ref[...].astype(F32)
    sites = res_ref.shape[1]
    wide = wide_ref[...]
    rights = []
    right_cot = right_cot_ref[...]
    for m in range(1, n):
        both = jnp.concatenate([other_ref[m - 1, :64, :], other_ref[m - 1, 64:128, :]], axis=1)
        rights.append(stack_right(both[factors:]))
        inward = [pair_cotangent(wide, diagonal(other_ref[m - 1, 128 + g * 32 : 160 + g * 32, :])) for g in range(2)]
        right_cot = right_cot + mm_nt(jnp.concatenate(inward, axis=0), spread_left(both[:factors], seqs))
    right = jnp.concatenate(rights, axis=0)
    back = back_ref[...] + sum_groups(mm_tn(right, cots_ref[block:, :]), seqs)
    tiles = []
    for g in range(8):
        t = back[:, g * 128 : (g + 1) * 128]
        t = t + pltpu.roll(t, 8, 1)
        tiles.append(t + pltpu.roll(t, 16, 1))
    back = jnp.concatenate(tiles, axis=1).astype(BF)
    r, c = ids((total, back.shape[1]))
    back = jnp.where(c % 32 == 24 + r // seqs, jnp.concatenate([back] * rows, axis=0), jnp.zeros((), BF))
    r, c = ids((factors, back.shape[1]))
    left_cot = mm_nt(ones_where(c // 32 == r), back)
    right_cot = right_cot.astype(BF).astype(F32)
    right_cot = jnp.concatenate([right_cot[:factors], right_cot[factors:]], axis=1)
    r, c = ids((seqs, total))
    seq_row = mm(jnp.broadcast_to(seq_f, (8, seqs)).astype(BF), ones_where(r == c % seqs))[0:1, :]
    r, c = ids((sites, total))
    res_row = mm(jnp.broadcast_to(res_f, (8, sites)).astype(BF), ones_where(r == c // seqs + own * rows))[0:1, :]
    proj_cot = (jnp.concatenate([left_cot, right_cot], axis=0) * (seq_row * res_row)).astype(BF)
    proj_cot_ref[...] = proj_cot
    lr_grad = mm(proj_cot, sec_ref[...]).astype(BF)
    grad_scr[1024:1088, :] = lr_grad[:, :128]
    grad_scr[1088:1152, :] = lr_grad[:, 128:]
    outer = mm(right, left_ref[...]).astype(BF)
    final = final_ref[...]
    for g in range(2 * (n - 1)):
        final = final + mm(outer_groups(outer, g), diagonal(pairs_ref[block + g * 32 : block + (g + 1) * 32, :]))
    for g in range(8):
        for b in range(4):
            at = (4 * g + b) * 32
            grad_scr[at : at + 32, :] = final[g * 32 : (g + 1) * 32, b * 128 : (b + 1) * 128].astype(BF)
    split_halves(core, keep_ref, send_ref, grad_scr)


def attention_kernel(
    where_ref, proj_cot_ref, adj_ref, w_ref, aff_ref, lrt_ref, nb_ref, q_ref, k_ref, v_ref, gate_ref, att_ref, p_ref,
    gated_ref, hat1_ref, rs1_ref, hat2_ref, rs2_ref,
    dx_ref, keep_ref, send_ref, grad_scr, *, seqs,
):
    core = where_ref[1]
    total, width = adj_ref.shape
    rows = total // seqs
    mask = head_mask(width)
    same = ones_where(mask)
    cot = mm_tn(proj_cot_ref[...], lrt_ref[...]).astype(BF).astype(F32)
    hat2 = hat2_ref[...]
    d_gain2 = jnp.sum(cot * hat2, axis=0, keepdims=True)
    d_bias2 = jnp.sum(cot, axis=0, keepdims=True)
    upd = adj_ref[...] + normal_back(cot * aff_ref[3:4, :], hat2, rs2_ref[...])

    def put(index, grad):
        grad = grad.astype(BF)
        grad_scr[2 * index * total : (2 * index + 1) * total, :] = grad[:, :128]
        grad_scr[(2 * index + 1) * total : (2 * index + 2) * total, :] = grad[:, 128:]

    upd_b = upd.astype(BF)
    d_gated = mm_nt(upd_b, w_ref[4]).astype(BF).astype(F32)
    put(4, mm_tn(gated_ref[...], upd_b))
    gate = gate_ref[...]
    d_att = d_gated * gate
    d_z = d_gated * att_ref[...] * gate * (1.0 - gate)
    d_gate_bias = jnp.sum(d_z, axis=0, keepdims=True)
    nb = nb_ref[...]
    d_zb = d_z.astype(BF)
    put(3, mm_tn(nb, d_zb))
    d_attb = d_att.astype(BF)
    p = p_ref[...]
    pb = p.astype(BF)
    d_p, d_v = [], []
    for i in range(rows):
        at = slice(i * seqs, (i + 1) * seqs)
        d_p.append(mm_nt(d_attb[at], spread_heads(v_ref[at, :], mask)))
        d_v.append(gather_heads(mm_tn(pb[at], d_attb[at]), mask))
    d_p = jnp.concatenate(d_p, axis=0).astype(BF).astype(F32)
    d_v = jnp.concatenate(d_v, axis=0).astype(BF)
    put(2, mm_tn(nb, d_v))
    d_s = (p * (d_p - group_sum(p * d_p, same))).astype(BF)
    d_q, d_k = [], []
    for i in range(rows):
        at = slice(i * seqs, (i + 1) * seqs)
        d_q.append(mm(d_s[at], spread_heads(k_ref[at, :], mask)))
        d_k.append(gather_heads(mm_tn(d_s[at], q_ref[at, :]), mask))
    d_q = jnp.concatenate(d_q, axis=0).astype(BF).astype(F32) * HEAD_DIM ** (-0.5)
    d_q = d_q.astype(BF)
    d_k = jnp.concatenate(d_k, axis=0).astype(BF)
    put(0, mm_tn(nb, d_q))
    put(1, mm_tn(nb, d_k))
    cot = mm_nt(d_q, w_ref[0]) + mm_nt(d_k, w_ref[1]) + mm_nt(d_v, w_ref[2]) + mm_nt(d_zb, w_ref[3])
    cot = cot.astype(BF).astype(F32)
    hat1 = hat1_ref[...]
    d_gain1 = jnp.sum(cot * hat1, axis=0, keepdims=True)
    d_bias1 = jnp.sum(cot, axis=0, keepdims=True)
    d_x = (upd + normal_back(cot * aff_ref[0:1, :], hat1, rs1_ref[...])).astype(BF)
    dx_ref[...] = mm_tn(to_residue_major(seqs, rows), d_x).astype(BF)
    vectors = jnp.concatenate(
        [d_gain1, d_bias1, d_gate_bias, d_gain2, d_bias2, jnp.zeros((3, width), F32)], axis=0
    )
    base = 10 * total
    grad_scr[base : base + 16, :] = jnp.concatenate([vectors[:, :128], vectors[:, 128:]], axis=0).astype(BF)
    grad_scr[base + 16 :, :] = jnp.zeros((grad_scr.shape[0] - base - 16, 128), BF)
    split_halves(core, keep_ref, send_ref, grad_scr)


def join_halves(core, mine_ref, other_ref, scr):
    half = mine_ref.shape[0]
    scr[pl.ds(pl.multiple_of(core * half, half), half), :] = mine_ref[...]
    scr[pl.ds(pl.multiple_of((1 - core) * half, half), half), :] = other_ref[...]


def unpack_pairs_kernel(where_ref, mine_ref, other_ref, lrt_ref, final_ref, scr):
    join_halves(where_ref[1], mine_ref, other_ref, scr)
    final_ref[...] = scr[:1024, :].astype(F32)
    lrt_ref[:, :128] = scr[1024:1088, :].astype(F32)
    lrt_ref[:, 128:] = scr[1088:1152, :].astype(F32)


def unpack_attention_kernel(where_ref, mine_ref, other_ref, att_ref, vec_ref, scr):
    join_halves(where_ref[1], mine_ref, other_ref, scr)
    total = att_ref.shape[1]
    for w in range(5):
        for h in range(2):
            at = (2 * w + h) * total
            att_ref[w, :, h * 128 : (h + 1) * 128] = scr[at : at + total, :].astype(F32)
    base = 10 * total
    vectors = scr[base : base + 16, :].astype(F32)
    vec_ref[:, :128] = vectors[:5]
    vec_ref[:, 128:] = vectors[8:13]


def call(kernel, outs, scratch, where, *args, space=pltpu.VMEM):
    return pl.pallas_call(
        kernel,
        out_shape=[jax.ShapeDtypeStruct(s, d) for s, d in outs],
        in_specs=[pl.BlockSpec(memory_space=pltpu.SMEM)] * len(where) + [pl.BlockSpec(memory_space=space)] * len(args),
        out_specs=[pl.BlockSpec(memory_space=pltpu.VMEM)] * len(outs),
        scratch_shapes=scratch,
        compiler_params=pltpu.CompilerParams(vmem_limit_bytes=24 * 1024 * 1024),
    )(*where, *[pltpu.with_memory_space_constraint(a, space) for a in args] if space != pltpu.VMEM else args)


def exchange(value, axes, total, offset):
    return lax.ppermute(value, axes, [(i, i ^ offset) for i in range(total)])


def reduce_gradients(keep, send, index, dp_size, axial_size):
    axes = ("dp", "axial")
    if axial_size != 2 or dp_size != 16:
        summed = lax.psum((keep.astype(F32), send.astype(F32)), axes)
        return summed[0].astype(BF), summed[1].astype(BF)
    total = dp_size * axial_size
    half = keep.shape[0]
    mine = keep.astype(F32) + exchange(send, axes, total, 2).astype(F32)
    place = (index % 2) + 2 * ((index // 4) % 2)
    offsets = (1, 4, 5)
    quarter = half // 4
    own = lax.dynamic_slice_in_dim(mine, place * quarter, quarter)
    got = []
    for step, offset in zip((1, 2, 3), offsets):
        piece = lax.dynamic_slice_in_dim(mine, (place ^ step) * quarter, quarter)
        got.append(exchange(piece.astype(BF), axes, total, offset))
    own = own + got[0].astype(F32) + got[1].astype(F32) + got[2].astype(F32)
    own = own.astype(BF)
    level = [exchange(own, axes, total, offset).astype(F32) for offset in (8, 16, 24)]
    own = ((own.astype(F32) + level[0]) + (level[1] + level[2])).astype(BF)
    pieces = [own] + [exchange(own, axes, total, offset) for offset in offsets]
    stacked = jnp.stack(pieces)
    mine = jnp.concatenate([lax.dynamic_index_in_dim(stacked, place ^ k, keepdims=False) for k in range(4)], axis=0)
    return mine, exchange(mine, axes, total, 2)


def per_device(
    dp_size,
    axial_size,
    homolog_activations,
    homolog_adjoint,
    duplex_adjoint,
    homolog_exists_filter,
    amino_exists_filter,
    focus_matrices_tier,
    affine_parameters,
    left_right_matrices,
    outer_final_matrix,
):
    n = axial_size
    _, seqs, rows, width = homolog_activations.shape
    total = seqs * rows
    index = lax.axis_index(("dp", "axial"))
    own = lax.axis_index("axial")
    fast = axial_size == 2 and dp_size == 16
    core = (index // 2) % 2 if fast else jnp.zeros_like(index)
    where = [jnp.stack([own, core])]
    x = homolog_activations.reshape(total, width)
    adj = homolog_adjoint.reshape(total, width)
    dup = duplex_adjoint.reshape(-1, DUPLEX_FEATURES)
    lrt = left_right_matrices.T
    flat_b, flat_f, column = ((total, width), BF), ((total, width), F32), ((total, 1), F32)
    block = rows * rows
    lanes = OUTER_FACTORS * 32
    inputs = (homolog_exists_filter, amino_exists_filter, focus_matrices_tier, affine_parameters, lrt, outer_final_matrix)
    results = call(
        partial(forward_kernel, n=n),
        [
            ((2 * OUTER_FACTORS, total), BF), ((n * block, DUPLEX_FEATURES), BF),
            flat_b, flat_b, flat_b, flat_b, flat_f, flat_f, flat_f, flat_b, flat_f, column, flat_f, column, flat_b,
            ((n - 1, 128 + block, DUPLEX_FEATURES), BF),
        ] + [(a.shape, a.dtype) for a in (*inputs, adj)],
        [pltpu.VMEM(x.shape, BF), pltpu.VMEM(dup.shape, BF), pltpu.VMEM(dup.shape, F32), pltpu.SemaphoreType.DMA((9,))],
        where, x, dup, *inputs, adj, space=pltpu.HBM,
    )
    proj, pairs, saved, messages = results[0], results[1], results[2:15], results[15]
    seq, res, w, aff, lrt, wf, adj = results[16:]
    others = [lax.ppermute(messages[m - 1], "axial", [(a, (a - m) % n) for a in range(n)]) for m in range(1, n)]
    near = call(
        partial(local_pairs_kernel, n=n),
        [
            ((n * block, lanes), BF), ((128, lanes), BF), ((seqs, lanes), F32), ((block, 128), F32), ((256, 512), F32),
            ((256, 512), BF), flat_f,
        ],
        [],
        [], proj, pairs, wf, seq, adj,
    )
    *near, adj = near
    half_pairs = (outer_final_matrix.shape[0] + 128) // 2
    proj_cot, keep, send = call(
        partial(pairs_kernel, n=n),
        [(proj.shape, BF), ((half_pairs, 128), BF), ((half_pairs, 128), BF)],
        [pltpu.VMEM((2 * half_pairs, 128), BF)],
        where, jnp.stack(others), pairs, *near, seq, res, saved[-1],
    )
    mine, other = reduce_gradients(keep, send, index, dp_size, axial_size)
    grad_lrt, grad_final = call(
        unpack_pairs_kernel,
        [(lrt.shape, F32), (outer_final_matrix.shape, F32)],
        [pltpu.VMEM((2 * half_pairs, 128), BF)],
        where, mine, other,
    )
    half = -(-(10 * total + 16) // 64) * 32
    dx, keep, send = call(
        partial(attention_kernel, seqs=seqs),
        [flat_b, ((half, 128), BF), ((half, 128), BF)],
        [pltpu.VMEM((2 * half, 128), BF)],
        where, proj_cot, adj, w, aff, lrt, *saved[:-1],
    )
    mine, other = reduce_gradients(keep, send, index, dp_size, axial_size)
    grad_att, grad_vec = call(
        unpack_attention_kernel,
        [(focus_matrices_tier.shape, F32), (affine_parameters.shape, F32)],
        [pltpu.VMEM((2 * half, 128), BF)],
        where, mine, other,
    )
    return (dx.reshape(homolog_activations.shape), grad_att, grad_vec, grad_lrt.T, grad_final)


def solution(mesh):
    return jax.shard_map(
        partial(per_device, mesh.shape["dp"], mesh.shape["axial"]),
        mesh=mesh,
        in_specs=(
            P("dp", None, "axial", None),
            P("dp", None, "axial", None),
            P("dp", "axial", None, None),
            P("dp", None),
            P("dp", None),
            P(),
            P(),
            P(),
            P(),
        ),
        out_specs=(P("dp", None, "axial", None), P(), P(), P(), P()),
        check_vma=False,
    )
```
